32 devices in a mesh: patch: 2 (over x), epoch: 16 (over z, y, core).
Axes of the slice: x: 2, y: 2, z: 4, core: 2. Of those that a mesh axis runs over, the one named last changes fastest.
Arguments:
- images: float32 [32, 128, 1024], P(('patch', 'epoch')), parts along dimension 0, may hold values from -20 to 20, as said below
- variance: float32 [32], P(('patch', 'epoch')), parts along dimension 0, may hold values from 0.25 to 4
- zero_point: float32 [32], P(('patch', 'epoch')), parts along dimension 0, may hold values from 0.5 to 2
- block_mask: int32 [32, 1], P(('patch', 'epoch')), parts along dimension 0, may hold values 0 or 1
- stamps: int32 [32, 512], P(('patch', 'epoch')), parts along dimension 0, may hold values from 0 to 131071
- owners: int32 [8], P('patch'), parts along dimension 0, may hold values from 0 to 15
Outputs:
- significance: float32 [32, 128, 1024], P(('patch', 'epoch')), parts along dimension 0
- coefficients: float32 [32, 15], P(('patch', 'epoch')), parts along dimension 0
The draws below stay inside these ranges and needn't reach their ends.
There are 2 independent parts, one for each index of `patch`. The reference program is written for one: setup_inputs(seed, part) draws one part's arguments, and reference() takes and returns one part's arrays. A program takes and returns all parts, laid end to end along the dimension named above; each array names one. Nothing has to cross between parts.
Inputs may be any that keep to these rules, and one draw needn't show every extreme that they name: `images`: each epoch is a common sky times an epoch scale plus noise.
All inputs are finite; a program needn't handle non-finite values. No bound on the sum of `block_mask` on one device may be relied on, other than what follows from the above.
Results may differ from the reference program's by a relative error of at most 0.00075.
The reference program's roundings to bfloat16 on the way count: a program that leaves them out, or rounds other values in their place, can miss the bound.
Values sent between devices are 32-bit elements; how exact they have to be, the bound alone decides.
A program may use at most 64 MiB of HBM per device.

```python
import math
import jax
import jax.numpy as jnp
from jax import lax

H = 128
W = 1024
TILES = 4
KHALF = 7
NBASIS = 12
NSTAMP = 512
NBLOCK = 1
EPOCHS = 16


def draw_images(key, part):
    sky = jnp.clip(jax.random.normal(jax.random.fold_in(key, 11), (H, W), jnp.float32), -6.0, 6.0)
    scales = jax.random.uniform(jax.random.fold_in(key, 12), (EPOCHS,), jnp.float32, 0.5, 1.5)
    noise = 0.3 * jnp.clip(jax.random.normal(jax.random.fold_in(key, 14), (EPOCHS, H, W), jnp.float32), -6.0, 6.0)
    return scales[:, None, None] * sky[None] + noise


def with_ends(drawn, stream_key, least, high):
    longest = drawn.shape.index(max(drawn.shape))
    spots = []
    for shift in (0, 1):
        where = [jax.random.randint(jax.random.fold_in(stream_key, axis), (), 0, length) for axis, length in enumerate(drawn.shape)]
        where[longest] = (where[longest] + shift) % drawn.shape[longest]
        spots.append(tuple(where))
    return drawn.at[spots[0]].set(least).at[spots[1]].set(high)


def block_levels(own_key, dims, pieces, smallest, top_value):
    factor_of, own = 1.0, jax.random.fold_in(own_key, 6)
    for dim, blocks in pieces:
        heights = jnp.exp(jax.random.uniform(jax.random.fold_in(own, dim), (blocks,), jnp.float32, smallest / len(pieces), top_value / len(pieces)))
        factor_of = factor_of * jnp.repeat(heights, dims[dim] // blocks).reshape([-1 if axis == dim else 1 for axis in range(len(dims))])
    return factor_of


def setup_inputs(seed: int = 0, part: int = 0) -> dict:
    seeds = jax.random.split(jax.random.key(seed), 7)
    part_splits = jax.random.split(jax.random.fold_in(seeds[6], part), 7)
    images = draw_images(jax.random.fold_in(jax.random.fold_in(seeds[6], part), 71), part)
    variance = jnp.clip(jnp.exp(math.log(4.0) - 2.7725887 * jax.random.uniform(part_splits[1], (EPOCHS,), jnp.float32) ** block_levels(part_splits[1], (EPOCHS,), ((0, 16),), -0.2, 0.2)), 0.25, 4.0)
    zero_point = jnp.clip(jnp.exp(math.log(2.0) - 1.3862944 * jax.random.uniform(part_splits[2], (EPOCHS,), jnp.float32) ** block_levels(part_splits[2], (EPOCHS,), ((0, 16),), -0.2, 0.2)), 0.5, 2.0)
    block_mask = with_ends((jax.random.randint(part_splits[3], (EPOCHS, NBLOCK), 0, 4) < 3).astype(jnp.int32), jax.random.fold_in(part_splits[3], 1), 0, 1)
    stamps = with_ends(jax.random.randint(part_splits[4], (EPOCHS, NSTAMP), 0, H * W), jax.random.fold_in(part_splits[4], 1), 0, (H * W) - 1).astype(jnp.int32)
    owners = with_ends(jax.random.randint(part_splits[5], (TILES,), 0, EPOCHS), jax.random.fold_in(part_splits[5], 1), 0, EPOCHS - 1).astype(jnp.int32)
    return {"images": images, "variance": variance, "zero_point": zero_point, "block_mask": block_mask, "stamps": stamps, "owners": owners}


sigma_list = (0.75, 1.5, 3.0)
basis_pairs = ((0, 0), (2, 0), (0, 2), (1, 1))

def raise_power(scaled, degree):
    result = jnp.ones_like(scaled)
    for step in range(degree):
        result = result * scaled
    return result

def tap_values(offset, sigma, degree):
    scaled = offset / sigma
    value = jnp.exp(-0.5 * scaled * scaled) * raise_power(scaled, degree) / (math.sqrt(2.0 * math.pi) * sigma)
    value = jnp.where(jnp.abs(offset) <= KHALF, value, 0.0)
    return value.astype(jnp.bfloat16)

def tap_vector(sigma, degree):
    offset = jnp.arange(-KHALF, KHALF + 1).astype(jnp.float32)
    return tap_values(offset, sigma, degree).astype(jnp.float32)

def correlate_cols(field, taps):
    padded = jnp.pad(field, ((0, 0), (KHALF, KHALF)))
    total = jnp.zeros(field.shape, jnp.float32)
    for shift in range(2 * KHALF + 1):
        total = total + taps[shift] * padded[:, shift:shift + field.shape[1]]
    return total

def correlate_rows(field, taps):
    padded = jnp.pad(field, ((KHALF, KHALF), (0, 0)))
    total = jnp.zeros(field.shape, jnp.float32)
    for shift in range(2 * KHALF + 1):
        total = total + taps[shift] * padded[shift:shift + field.shape[0], :]
    return total

def one_epoch(image, stamp_row, mask_row, reference_img):
    sharp = lax.optimization_barrier(image.astype(jnp.bfloat16)).astype(jnp.float32)
    bases = []
    for sigma in sigma_list:
        across = {}
        for degree in (0, 1, 2):
            temp = correlate_cols(sharp, tap_vector(sigma, degree)).astype(jnp.bfloat16)
            across[degree] = lax.optimization_barrier(temp).astype(jnp.float32)
        for pair in basis_pairs:
            bases.append(correlate_rows(across[pair[0]], tap_vector(sigma, pair[1])).astype(jnp.bfloat16))
    xn = 2.0 * (jnp.arange(W).astype(jnp.float32) + 0.5) / W - 1.0
    yn = 2.0 * (jnp.arange(H).astype(jnp.float32) + 0.5) / H - 1.0
    cols = stamp_row % W
    rows = stamp_row // W
    picks = [jnp.take(b.reshape(-1), stamp_row).astype(jnp.float32) for b in bases]
    picks = picks + [jnp.ones((NSTAMP,), jnp.float32), xn[cols], yn[rows]]
    design = jnp.stack(picks, axis=0)
    normal = jnp.dot(design, design.T, precision=lax.Precision.HIGHEST)
    normal = normal + 0.05 * jnp.diag(jnp.diag(normal))
    rhs = jnp.dot(design, jnp.take(reference_img.reshape(-1), stamp_row), precision=lax.Precision.HIGHEST)
    factor = jnp.linalg.cholesky(normal)
    coef = jax.scipy.linalg.cho_solve((factor, True), rhs)
    model = jnp.zeros((H, W), jnp.float32)
    for index in range(NBASIS):
        model = model + coef[index] * bases[index].astype(jnp.float32)
    model = model + coef[NBASIS] + coef[NBASIS + 1] * xn[None, :] + coef[NBASIS + 2] * yn[:, None]
    pixel_mask = jnp.repeat(mask_row.astype(jnp.float32), 128)
    diff = pixel_mask[:, None] * (model - reference_img)
    return (diff, coef)

def reference(images, variance, zero_point, block_mask, stamps, owners):
    weight = 1.0 / variance
    block_w = weight[:, None] * block_mask.astype(jnp.float32)
    row_w = jnp.repeat(block_w, 128, axis=1)
    numerator = jnp.einsum('ey,eyx->yx', row_w, images, precision=lax.Precision.HIGHEST)
    denominator = 1.0 + lax.optimization_barrier(jnp.sum(block_w, axis=0))
    owner_scale = lax.optimization_barrier(jnp.sum((owners[:, None] == jnp.arange(EPOCHS)[None, :]).astype(jnp.float32) * zero_point[None, :], axis=1))
    col_scale = jnp.repeat(owner_scale, W // TILES)
    den_rows = jnp.repeat(denominator, 128)
    reference_img = numerator / den_rows[:, None] * col_scale[None, :]
    diffs, coefs = lax.map(lambda item: one_epoch(item[0], item[1], item[2], reference_img), (images, stamps, block_mask))
    pooled = lax.optimization_barrier(jnp.sum(diffs * diffs, axis=0))
    scatter = jnp.sqrt(0.05 + pooled / EPOCHS)
    return (diffs / scatter[None], coefs)
```

```python
import functools
import math

import jax
import jax.numpy as jnp
from jax import lax
from jax.experimental import pallas as pl
from jax.experimental.pallas import tpu as pltpu
from jax.sharding import PartitionSpec as P

TILES = 4
KHALF = 7
NBASIS = 12
LANES = 128

sigma_list = (0.75, 1.5, 3.0)
basis_pairs = ((0, 0), (2, 0), (0, 2), (1, 1))
MESH = pl.DeviceIdType.MESH


def tap_values(offset, sigma, degree):
    scaled = offset / sigma
    power = jnp.ones_like(scaled)
    for _ in range(degree):
        power = power * scaled
    value = jnp.exp(-0.5 * scaled * scaled) * power / (math.sqrt(2.0 * math.pi) * sigma)
    return jnp.where(jnp.abs(offset) <= KHALF, value, 0.0).astype(jnp.bfloat16)


def kernel(
    count, height, width, stripes,
    image_in, var_ref, zp_ref, mask_ref, owner_in, stamp_in,
    diff_ref, inv_ref, coef_ref,
    x1, x2, g1, g2, ra1, ra2, rd1, rd2,
    s_own, s_mid, sa, sd,
    lhs, across, bases, onehot, design, hits,
    image_ref, owner_ref, stamp_ref, load,
    send1, recv1, send2, recv2, send3, recv3,
):
    chips = count // 2
    _, pr, pc = x1.shape
    subs = width // (pc * stripes)
    pcc = pc * stripes
    npix = stamp_ref.shape[1]
    half_rows = height // 2

    me = lax.axis_index("epoch")
    core = lax.rem(me, 2)
    chip = me // 2
    power = chips & (chips - 1) == 0

    def device(which, cc):
        return {"epoch": which * 2 + cc}

    def to(j):
        if not power:
            return lax.rem(chip + j, chips)
        value, bit = chip, 1
        while bit <= j:
            if j & bit:
                value = value + bit * (1 - 2 * lax.rem(chip // bit, 2))
            bit *= 2
        return value

    def source(j):
        return to(j) if power else lax.rem(chip - j + chips, chips)

    order = list(range(chips - 1, 0, -1))
    mate = device(chip, 1 - core)
    peers = [mate] + [device(to(j), core) for j in order]

    barrier = pltpu.get_barrier_semaphore()
    for peer in peers:
        pl.semaphore_signal(barrier, inc=1, device_id=peer, device_id_type=MESH)

    loads = [
        pltpu.make_async_copy(src, dst, load.at[i])
        for i, (src, dst) in enumerate(((image_in, image_ref), (owner_in, owner_ref), (stamp_in, stamp_ref)))
    ]
    for copy in loads:
        copy.start()

    pending = []

    class Lane:
        def __init__(self, send, recv):
            self.send, self.recv, self.next = send, recv, 0

        def start(self, src, dst, device_id):
            copy = pltpu.make_async_remote_copy(
                src_ref=src, dst_ref=dst, send_sem=self.send.at[self.next], recv_sem=self.recv.at[self.next],
                device_id=device_id, device_id_type=MESH,
            )
            self.next += 1
            copy.start()
            pending.append(copy)
            return copy

    def first(s, side):
        return (s * 2 + side) * chips

    class Reduce:
        def __init__(self, x, g, ra, rd, lane):
            self.x, self.g, self.ra, self.rd, self.lane = x, g, ra, rd, lane
            self.at = {}

        def swap(self, s):
            self.at["a", s] = self.lane.start(
                self.x.at[pl.ds(first(s, 1 - core), chips)], self.ra.at[pl.ds(s * chips, chips)], mate
            )

        def scatter(self, s):
            self.at["a", s].wait_recv()
            for j in order:
                dest = to(j)
                own = first(s, core) + dest
                self.x[own] = self.x[own] + self.ra[s * chips + dest]
                self.at["b", s, j] = self.lane.start(
                    self.x.at[own], self.rd.at[s * chips + j], device(dest, core)
                )

        def settle(self, s, final):
            own = first(s, core) + chip
            total = self.x[own] + self.ra[s * chips + chip]
            for j in order[::-1]:
                self.at["b", s, j].wait_recv()
                total = total + self.rd[s * chips + j]
            self.g[own] = final(s, total)
            for j in order:
                self.at["d", s, j] = self.lane.start(self.g.at[own], self.g.at[own], device(to(j), core))
            self.at["e", s, 0] = self.lane.start(self.g.at[own], self.g.at[own], mate)

        def hand(self, s):
            for j in order[::-1]:
                self.at["d", s, j].wait_recv()
                block = self.g.at[first(s, core) + source(j)]
                self.at["e", s, j] = self.lane.start(block, block, mate)

        def end(self, s):
            for j in range(chips):
                self.at["e", s, j].wait_recv()

    def columns(s, sub):
        return sub * pcc + s * pc

    def piece(s, gi, sub):
        return 2 * chips * s + gi * subs + sub

    one = Reduce(x1, g1, ra1, rd1, Lane(send1, recv1))
    two = Reduce(x2, g2, ra2, rd2, Lane(send2, recv2))
    tiny = Lane(send3, recv3)

    weight = 1.0 / jnp.full((8, LANES), var_ref[0], jnp.float32)
    mask = jnp.full((8, LANES), mask_ref[0, 0].astype(jnp.float32), jnp.float32)
    block_term = weight * mask
    term = block_term[0:1, 0:1]
    lane = lax.broadcasted_iota(jnp.int32, (8, LANES), 1)
    loads[1].wait()
    small = jnp.where(lane == TILES, block_term, 0.0)
    for t in range(TILES):
        value = jnp.where(owner_ref[t] == me, zp_ref[0], 0.0)
        small = small + jnp.where(lane == t, value, 0.0)
    s_own[...] = small
    loads[0].wait()
    for s in range(stripes):
        for gi in range(height // pr):
            for sub in range(subs):
                c0 = columns(s, sub)
                x1[piece(s, gi, sub)] = image_ref[0, gi * pr:(gi + 1) * pr, c0:c0 + pc] * term

    pl.semaphore_wait(barrier, len(peers))
    tiny_a = tiny.start(s_own, sa, mate)
    for s in range(stripes):
        one.swap(s)

    sharp = image_ref[0].astype(jnp.bfloat16)
    ntile = width // LANES
    zero = jnp.zeros((height, LANES), jnp.bfloat16)

    def spread():
        for t in range(ntile):
            for s in range(3):
                src = t + s - 1
                value = sharp[:, src * LANES:(src + 1) * LANES] if 0 <= src < ntile else zero
                lhs[t * height:(t + 1) * height, s * LANES:(s + 1) * LANES] = value

    off_h = (
        lax.broadcasted_iota(jnp.int32, (3 * LANES, LANES), 0)
        - LANES
        - lax.broadcasted_iota(jnp.int32, (3 * LANES, LANES), 1)
    ).astype(jnp.float32)
    off_v = (
        lax.broadcasted_iota(jnp.int32, (height, height), 1) - lax.broadcasted_iota(jnp.int32, (height, height), 0)
    ).astype(jnp.float32)

    def horizontal(si):
        sigma = sigma_list[si]
        band = jnp.concatenate([tap_values(off_h, sigma, degree) for degree in (0, 1, 2)], axis=1)
        for t in range(0, ntile, 2):
            res = jnp.dot(
                lhs[t * height:(t + 2) * height, :], band, preferred_element_type=jnp.float32
            ).astype(jnp.bfloat16)
            for u in range(2):
                for degree in (0, 1, 2):
                    across[si * 3 + degree, :, (t + u) * LANES:(t + u + 1) * LANES] = res[
                        u * height:(u + 1) * height, degree * LANES:(degree + 1) * LANES
                    ]

    def vertical(si):
        sigma = sigma_list[si]
        bands = [tap_values(off_v, sigma, degree) for degree in (0, 1, 2)]
        for i, j in basis_pairs:
            k = si * 4 + basis_pairs.index((i, j))
            bases[k * height:(k + 1) * height, :] = jnp.dot(
                bands[j], across[si * 3 + i], preferred_element_type=jnp.float32
            ).astype(jnp.bfloat16)

    state = {}

    def stamped():
        loads[2].wait()
        stamp = stamp_ref[...]
        shift = width.bit_length() - 1
        rows = lax.shift_right_logical(stamp, shift)
        cols = stamp - lax.shift_left(rows, shift)
        onehot[...] = jnp.where(
            lax.broadcasted_iota(jnp.int32, (width, npix), 0) == cols, 1.0, 0.0
        ).astype(jnp.bfloat16)
        row_hit = lax.broadcasted_iota(jnp.int32, (height, npix), 0) == rows
        state["hit"] = row_hit
        hits[...] = lax.dot_general(
            jnp.where(row_hit, 1.0, 0.0).astype(jnp.bfloat16), onehot[...], (((1,), (1,)), ((), ())),
            preferred_element_type=jnp.float32,
        )
        design[...] = jnp.zeros_like(design)
        design[16 + NBASIS:17 + NBASIS, :] = jnp.ones((1, npix), jnp.float32)
        design[17 + NBASIS:18 + NBASIS, :] = 2.0 * (cols.astype(jnp.float32) + 0.5) / width - 1.0
        design[18 + NBASIS:19 + NBASIS, :] = 2.0 * (rows.astype(jnp.float32) + 0.5) / height - 1.0

    def pick(k):
        got = jnp.dot(
            bases[k * height:(k + 1) * height, :], onehot[...], preferred_element_type=jnp.float32
        )
        design[16 + k:17 + k, :] = jnp.sum(jnp.where(state["hit"], got, 0.0), axis=0, keepdims=True)

    def invert():
        rowi = lax.broadcasted_iota(jnp.int32, (16, LANES), 0)
        lanei = lax.broadcasted_iota(jnp.int32, (16, LANES), 1)
        normal = lax.dot_general(
            design[16:32, :], design[...], (((1,), (1,)), ((), ())),
            precision=lax.Precision.HIGHEST, preferred_element_type=jnp.float32,
        )
        aug = jnp.where(lanei == rowi + 16, normal + 0.05 * normal, normal)
        aug = jnp.where(lanei == rowi, 1.0, aug)
        aug = jnp.where((rowi == 15) & (lanei == 31), 1.0, aug)
        for k in range(NBASIS + 3):
            row = aug[k:k + 1, :] / aug[k:k + 1, 16 + k:17 + k]
            aug = jnp.where(rowi == k, row, aug - aug[:, 16 + k:17 + k] * row)
        state["aug"] = aug

    def sums():
        for copy in tiny_b:
            copy.wait_recv()
        total = s_mid[...]
        for j in order:
            total = total + sd[j]
        state["denom"] = 1.0 + total[:, TILES:TILES + 1]
        state["total"] = total

    def make_reference(s, numer):
        total = state["total"]
        col = lax.broadcasted_iota(jnp.int32, (pr, pc), 1) + s * pc
        if subs > 1:
            col = col + lax.rem(core * chips + chip, subs) * pcc
        scale = jnp.broadcast_to(total[:1, 0:1], (pr, pc))
        for t in range(1, TILES):
            scale = jnp.where(
                col >= t * (width // TILES), jnp.broadcast_to(total[:1, t:t + 1], (pr, pc)), scale
            )
        return numer / jnp.broadcast_to(state["denom"][:1], (pr, pc)) * scale

    xn = 2.0 * (lax.broadcasted_iota(jnp.int32, (1, width), 1).astype(jnp.float32) + 0.5) / width - 1.0
    span = max(16, pr)

    def xn_of(c0):
        return 2.0 * ((lax.broadcasted_iota(jnp.int32, (1, pc), 1) + c0).astype(jnp.float32) + 0.5) / width - 1.0

    def yn_of(row):
        return 2.0 * ((lax.broadcasted_iota(jnp.int32, (span, 1), 0) + row).astype(jnp.float32) + 0.5) / height - 1.0

    def fold(value):
        total = value[0:8, 0:LANES]
        for r in range(0, value.shape[0], 8):
            for c in range(0, value.shape[1], LANES):
                if r or c:
                    total = total + value[r:r + 8, c:c + LANES]
        return total

    def patch(ref, s, r0, sub):
        rows = [ref[piece(s, r0 // pr + q, sub)] for q in range(span // pr)]
        return rows[0] if len(rows) == 1 else jnp.concatenate(rows, axis=0)

    acc = [jnp.zeros((8, LANES), jnp.float32) for _ in range(NBASIS + 3)]

    def project(s):
        for r0 in range(0, height, span):
            for sub in range(subs):
                c0 = columns(s, sub)
                part = patch(g1, s, r0, sub) * hits[r0:r0 + span, c0:c0 + pc]
                for k in range(NBASIS):
                    base = bases[k * height + r0:k * height + r0 + span, c0:c0 + pc].astype(jnp.float32)
                    acc[k] = acc[k] + fold(part * base)
                acc[NBASIS] = acc[NBASIS] + fold(part)
                acc[NBASIS + 1] = acc[NBASIS + 1] + fold(part * xn_of(c0))
                acc[NBASIS + 2] = acc[NBASIS + 2] + fold(part * yn_of(r0))

    def solve():
        rows = [jnp.sum(value, axis=0, keepdims=True) for value in acc]
        rows.append(jnp.zeros((1, LANES), jnp.float32))
        rhs = jnp.sum(jnp.concatenate(rows, axis=0), axis=1, keepdims=True)
        coef = jnp.sum(state["aug"] * rhs, axis=0, keepdims=True)
        coef_ref[...] = coef[:, 0:NBASIS + 3]
        state["coefs"] = [coef[:, k:k + 1] for k in range(NBASIS + 3)]

    mask_one = mask[0:1, 0:1]

    def residual(s, side):
        coefs = state["coefs"]
        for r0 in range(0, half_rows, span):
            row = pl.multiple_of(side * half_rows + r0, span)
            for sub in range(subs):
                c0 = columns(s, sub)
                model = coefs[NBASIS] + coefs[NBASIS + 1] * xn_of(c0) + coefs[NBASIS + 2] * yn_of(row)
                for k in range(NBASIS):
                    model = model + coefs[k] * bases[
                        pl.ds(pl.multiple_of(k * height + row, span), span), c0:c0 + pc
                    ].astype(jnp.float32)
                for q in range(span // pr):
                    at = piece(s, row // pr + q, sub)
                    diff = mask_one * (model[q * pr:(q + 1) * pr, :] - g1[at])
                    diff_ref[pl.ds(pl.multiple_of(row + q * pr, pr), pr), c0:c0 + pc] = diff
                    x2[at] = diff * diff

    def root(s, pooled):
        return 1.0 / jnp.sqrt(0.05 + pooled / count)

    spread()
    horizontal(0)
    tiny_a.wait_recv()
    s_mid[...] = s_own[...] + sa[...]
    tiny_b = [tiny.start(s_mid, sd.at[j], device(to(j), core)) for j in order]
    for s in range(stripes):
        one.scatter(s)
    horizontal(1)
    horizontal(2)
    for si in range(3):
        vertical(si)
    stamped()
    sums()
    for s in range(stripes):
        one.settle(s, make_reference)
        for k in range(s * NBASIS // stripes, (s + 1) * NBASIS // stripes):
            pick(k)
    invert()
    for s in range(stripes):
        one.hand(s)
    for s in range(stripes):
        one.end(s)
        project(s)
    solve()
    for s in range(stripes):
        residual(s, 1 - core)
        two.swap(s)
    for s in range(stripes):
        residual(s, core)
        two.scatter(s)
    for s in range(stripes):
        two.settle(s, root)
    for s in range(stripes):
        two.hand(s)
    for s in range(stripes):
        two.end(s)
        for gi in range(height // pr):
            for sub in range(subs):
                c0 = columns(s, sub)
                inv_ref[gi * pr:(gi + 1) * pr, c0:c0 + pc] = g2[piece(s, gi, sub)]
    for copy in pending:
        copy.wait_send()


def finish(diff_ref, inv_ref, coef_in, out_ref, coef_ref):
    out_ref[0] = diff_ref[...] * inv_ref[...]
    coef_ref[...] = coef_in[...]


def shards(images, variance, zero_point, block_mask, stamps, owners):
    _, height, width = images.shape
    count = lax.axis_size("epoch")
    chips = count // 2
    npix = stamps.shape[1]
    pr = max(8, height // count)
    pcc = width * height // (count * pr)
    stripes = 1
    while stripes < 2 and pcc // (stripes * 2) % LANES == 0:
        stripes *= 2
    pc = pcc // stripes
    f32 = jnp.float32
    big = pltpu.VMEM((stripes * count, pr, pc), f32)
    part = pltpu.VMEM((stripes * chips, pr, pc), f32)
    tile = pltpu.VMEM((8, LANES), f32)
    nsem = stripes * (1 + 2 * (chips - 1) + chips)
    dma = pltpu.SemaphoreType.DMA
    vmem = pl.BlockSpec(memory_space=pltpu.VMEM)
    smem = pl.BlockSpec(memory_space=pltpu.SMEM)
    hbm = pl.BlockSpec(memory_space=pltpu.HBM)
    images, owners, stamps = [pltpu.with_memory_space_constraint(v, pltpu.HBM) for v in (images, owners, stamps)]
    diff, inv, coef = pl.pallas_call(
        functools.partial(kernel, count, height, width, stripes),
        out_shape=(
            jax.ShapeDtypeStruct((height, width), f32),
            jax.ShapeDtypeStruct((height, width), f32),
            jax.ShapeDtypeStruct((1, NBASIS + 3), f32),
        ),
        in_specs=[hbm, smem, smem, smem, hbm, hbm],
        out_specs=(vmem,) * 3,
        scratch_shapes=[
            big, big, big, big, part, part, part, part,
            tile, tile, tile, pltpu.VMEM((chips, 8, LANES), f32),
            pltpu.VMEM((width // LANES * height, 3 * LANES), jnp.bfloat16),
            pltpu.VMEM((9, height, width), jnp.bfloat16),
            pltpu.VMEM((NBASIS * height, width), jnp.bfloat16),
            pltpu.VMEM((width, npix), jnp.bfloat16),
            pltpu.VMEM((LANES, npix), f32),
            pltpu.VMEM((height, width), f32),
            pltpu.VMEM(images.shape, f32),
            pltpu.SMEM(owners.shape, jnp.int32),
            pltpu.VMEM(stamps.shape, jnp.int32), dma((3,)),
            dma((nsem,)), dma((nsem,)), dma((nsem,)), dma((nsem,)), dma((chips,)), dma((chips,)),
        ],
        compiler_params=pltpu.CompilerParams(
            collective_id=0, has_side_effects=True, vmem_limit_bytes=40 * 1024 * 1024
        ),
    )(images, variance, zero_point, block_mask, owners, stamps)
    return pl.pallas_call(
        finish,
        out_shape=(
            jax.ShapeDtypeStruct((1, height, width), f32),
            jax.ShapeDtypeStruct((1, NBASIS + 3), f32),
        ),
        in_specs=[vmem] * 3,
        out_specs=(vmem,) * 2,
        compiler_params=pltpu.CompilerParams(vmem_limit_bytes=8 * 1024 * 1024),
    )(diff, inv, coef)


def solution(mesh):
    in_specs = (
        P(("patch", "epoch"), None, None),
        P(("patch", "epoch")),
        P(("patch", "epoch")),
        P(("patch", "epoch"), None),
        P(("patch", "epoch"), None),
        P("patch"),
    )
    out_specs = (P(("patch", "epoch"), None, None), P(("patch", "epoch"), None))
    return jax.shard_map(shards, mesh=mesh, in_specs=in_specs, out_specs=out_specs, check_vma=False)
```

```python
import functools
import math

import jax
import jax.numpy as jnp
from jax import lax
from jax.experimental import pallas as pl
from jax.experimental.pallas import tpu as pltpu
from jax.sharding import PartitionSpec as P

TILES = 4
KHALF = 7
NBASIS = 12
LANES = 128

sigma_list = (0.75, 1.5, 3.0)
basis_pairs = ((0, 0), (2, 0), (0, 2), (1, 1))
MESH = pl.DeviceIdType.MESH


def tap_values(offset, sigma, degree):
    scaled = offset / sigma
    power = jnp.ones_like(scaled)
    for _ in range(degree):
        power = power * scaled
    value = jnp.exp(-0.5 * scaled * scaled) * power / (math.sqrt(2.0 * math.pi) * sigma)
    return jnp.where(jnp.abs(offset) <= KHALF, value, 0.0).astype(jnp.bfloat16)


def kernel(
    count, height, width, stripes,
    image_in, var_ref, zp_ref, mask_ref, owner_in, stamp_in,
    diff_ref, inv_ref, coef_ref,
    x1, x2, g1, g2, ra1, ra2, rd1, rd2, rx1, rx2,
    s_own, s_mid, s_near, sa, sd, sx,
    lhs, across, bases, onehot, design, hits,
    image_ref, owner_ref, stamp_ref, load,
    send1, recv1, send2, recv2, send3, recv3, told,
):
    chips = count // 2
    _, pr, pc = x1.shape
    subs = width // (pc * stripes)
    pcc = pc * stripes
    npix = stamp_ref.shape[1]
    half_rows = height // 2

    me = lax.axis_index("epoch")
    core = lax.rem(me, 2)
    chip = me // 2
    near = chips // 2

    def device(which, cc):
        return {"epoch": which * 2 + cc}

    def to(j):
        value, bit = chip, 1
        while bit <= j:
            if j & bit:
                value = value + bit * (1 - 2 * lax.rem(chip // bit, 2))
            bit *= 2
        return value

    order = list(range(near - 1, 0, -1))
    mate = device(chip, 1 - core)
    slot = lax.rem(chip, near)

    barrier = pltpu.get_barrier_semaphore()

    @pl.when(core == 1)
    def _():
        pl.semaphore_signal(barrier, inc=1, device_id=mate, device_id_type=MESH)

    for j in order + [near]:
        pl.semaphore_signal(barrier, inc=1, device_id=device(to(j), 1), device_id_type=MESH)

    def enter_mate():
        @pl.when(core == 0)
        def _():
            pl.semaphore_wait(barrier, 1)
            pl.semaphore_signal(told, inc=1, device_id=mate, device_id_type=MESH)

        @pl.when(core == 1)
        def _():
            pl.semaphore_wait(told, 1)

    def enter_chips():
        @pl.when(core == 1)
        def _():
            pl.semaphore_wait(barrier, 2 * near)
            pl.semaphore_signal(told, inc=1, device_id=mate, device_id_type=MESH)

        @pl.when(core == 0)
        def _():
            pl.semaphore_wait(told, 1)

    def half_of(side):
        return pl.ds(pl.multiple_of(side * half_rows, 8), half_rows)

    loads = [
        pltpu.make_async_copy(src, dst, load.at[i])
        for i, (src, dst) in enumerate((
            (image_in.at[0, half_of(1 - core)], image_ref.at[0, half_of(1 - core)]), (owner_in, owner_ref),
            (image_in.at[0, half_of(core)], image_ref.at[0, half_of(core)]), (stamp_in, stamp_ref),
        ))
    ]
    for copy in loads:
        copy.start()

    pending = []

    class Lane:
        def __init__(self, send, recv):
            self.send, self.recv, self.next = send, recv, 0

        def start(self, src, dst, device_id):
            copy = pltpu.make_async_remote_copy(
                src_ref=src, dst_ref=dst, send_sem=self.send.at[self.next], recv_sem=self.recv.at[self.next],
                device_id=device_id, device_id_type=MESH,
            )
            self.next += 1
            copy.start()
            pending.append(copy)
            return copy

    def first(s, side):
        return (s * 2 + side) * near

    class Reduce:
        def __init__(self, x, g, ra, rd, rx, lane):
            self.x, self.g, self.ra, self.rd, self.rx, self.lane = x, g, ra, rd, rx, lane
            self.at = {}

        def swap(self, s):
            self.at["a", s] = self.lane.start(
                self.x.at[pl.ds(first(s, 1 - core), near)], self.ra.at[pl.ds(s * near, near)], mate
            )

        def merge(self, s):
            self.at["a", s].wait_recv()
            for c in range(near):
                own = first(s, core) + c
                self.x[own] = self.x[own] + self.ra[s * near + c]

        def scatter(self, s):
            for j in order:
                self.at["b", s, j] = self.lane.start(
                    self.x.at[first(s, core) + lax.rem(to(j), near)], self.rd.at[s * near + j], device(to(j), core)
                )

        def cross(self, s):
            own = first(s, core) + slot
            total = self.x[own]
            for j in order[::-1]:
                self.at["b", s, j].wait_recv()
                total = total + self.rd[s * near + j]
            self.x[own] = total
            self.at["c", s] = self.lane.start(self.x.at[own], self.rx.at[s], device(to(near), core))

        def settle(self, s, final):
            own = first(s, core) + slot
            self.at["c", s].wait_recv()
            self.g[own] = final(s, self.x[own] + self.rx[s])
            for j in order:
                self.at["d", s, j] = self.lane.start(self.g.at[own], self.g.at[own], device(to(j), core))
            block = self.g.at[pl.ds(own, 1)]
            self.at["e", s, 0] = self.lane.start(block, block, mate)

        def hand(self, s):
            for j in range(1, near):
                self.at["d", s, j].wait_recv()
                if j % 2:
                    where = lax.rem(to(j), near)
                    start = where if j == 1 else where // 2 * 2
                    block = self.g.at[pl.ds(first(s, core) + start, 1 if j == 1 else 2)]
                    self.at["e", s, j] = self.lane.start(block, block, mate)

        def end(self, s):
            for j in [0] + list(range(1, near, 2)):
                self.at["e", s, j].wait_recv()

    def columns(s, sub):
        return sub * pcc + s * pc

    def piece(s, gi, sub):
        return 2 * near * s + gi * subs + sub

    one = Reduce(x1, g1, ra1, rd1, rx1, Lane(send1, recv1))
    two = Reduce(x2, g2, ra2, rd2, rx2, Lane(send2, recv2))
    tiny = Lane(send3, recv3)

    weight = 1.0 / jnp.full((8, LANES), var_ref[0], jnp.float32)
    mask = jnp.full((8, LANES), mask_ref[0, 0].astype(jnp.float32), jnp.float32)
    block_term = weight * mask
    term = block_term[0:1, 0:1]
    lane = lax.broadcasted_iota(jnp.int32, (8, LANES), 1)
    loads[1].wait()
    small = jnp.where(lane == TILES, block_term, 0.0)
    for t in range(TILES):
        value = jnp.where(owner_ref[t] == me, zp_ref[0], 0.0)
        small = small + jnp.where(lane == t, value, 0.0)
    s_own[...] = small

    def weigh(s, side):
        for r0 in range(0, half_rows, pr):
            row = pl.multiple_of(side * half_rows + r0, pr)
            for sub in range(subs):
                c0 = columns(s, sub)
                x1[piece(s, row // pr, sub)] = image_ref[0, pl.ds(row, pr), c0:c0 + pc] * term

    ntile = width // LANES
    zero = jnp.zeros((height, LANES), jnp.bfloat16)

    def spread():
        sharp = image_ref[0].astype(jnp.bfloat16)
        for t in range(ntile):
            for s in range(3):
                src = t + s - 1
                value = sharp[:, src * LANES:(src + 1) * LANES] if 0 <= src < ntile else zero
                lhs[t * height:(t + 1) * height, s * LANES:(s + 1) * LANES] = value

    off_h = (
        lax.broadcasted_iota(jnp.int32, (3 * LANES, LANES), 0)
        - LANES
        - lax.broadcasted_iota(jnp.int32, (3 * LANES, LANES), 1)
    ).astype(jnp.float32)
    off_v = (
        lax.broadcasted_iota(jnp.int32, (height, height), 1) - lax.broadcasted_iota(jnp.int32, (height, height), 0)
    ).astype(jnp.float32)

    def horizontal(si):
        sigma = sigma_list[si]
        band = jnp.concatenate([tap_values(off_h, sigma, degree) for degree in (0, 1, 2)], axis=1)
        for t in range(0, ntile, 2):
            res = jnp.dot(
                lhs[t * height:(t + 2) * height, :], band, preferred_element_type=jnp.float32
            ).astype(jnp.bfloat16)
            for u in range(2):
                for degree in (0, 1, 2):
                    across[si * 3 + degree, :, (t + u) * LANES:(t + u + 1) * LANES] = res[
                        u * height:(u + 1) * height, degree * LANES:(degree + 1) * LANES
                    ]

    def vertical(si):
        sigma = sigma_list[si]
        bands = [tap_values(off_v, sigma, degree) for degree in (0, 1, 2)]
        for i, j in basis_pairs:
            k = si * 4 + basis_pairs.index((i, j))
            bases[k * height:(k + 1) * height, :] = jnp.dot(
                bands[j], across[si * 3 + i], preferred_element_type=jnp.float32
            ).astype(jnp.bfloat16)

    state = {}

    def stamped():
        loads[3].wait()
        stamp = stamp_ref[...]
        shift = width.bit_length() - 1
        rows = lax.shift_right_logical(stamp, shift)
        cols = stamp - lax.shift_left(rows, shift)
        onehot[...] = jnp.where(
            lax.broadcasted_iota(jnp.int32, (width, npix), 0) == cols, 1.0, 0.0
        ).astype(jnp.bfloat16)
        row_hit = lax.broadcasted_iota(jnp.int32, (height, npix), 0) == rows
        state["hit"] = row_hit
        hits[...] = lax.dot_general(
            jnp.where(row_hit, 1.0, 0.0).astype(jnp.bfloat16), onehot[...], (((1,), (1,)), ((), ())),
            preferred_element_type=jnp.float32,
        )
        design[...] = jnp.zeros_like(design)
        design[16 + NBASIS:17 + NBASIS, :] = jnp.ones((1, npix), jnp.float32)
        design[17 + NBASIS:18 + NBASIS, :] = 2.0 * (cols.astype(jnp.float32) + 0.5) / width - 1.0
        design[18 + NBASIS:19 + NBASIS, :] = 2.0 * (rows.astype(jnp.float32) + 0.5) / height - 1.0

    def pick(k):
        got = jnp.dot(
            bases[k * height:(k + 1) * height, :], onehot[...], preferred_element_type=jnp.float32
        )
        design[16 + k:17 + k, :] = jnp.sum(jnp.where(state["hit"], got, 0.0), axis=0, keepdims=True)

    def invert():
        rowi = lax.broadcasted_iota(jnp.int32, (16, LANES), 0)
        lanei = lax.broadcasted_iota(jnp.int32, (16, LANES), 1)
        normal = lax.dot_general(
            design[16:32, :], design[...], (((1,), (1,)), ((), ())),
            precision=lax.Precision.HIGHEST, preferred_element_type=jnp.float32,
        )
        aug = jnp.where(lanei == rowi + 16, normal + 0.05 * normal, normal)
        aug = jnp.where(lanei == rowi, 1.0, aug)
        aug = jnp.where((rowi == 15) & (lanei == 31), 1.0, aug)
        for k in range(NBASIS + 3):
            row = aug[k:k + 1, :] / aug[k:k + 1, 16 + k:17 + k]
            aug = jnp.where(rowi == k, row, aug - aug[:, 16 + k:17 + k] * row)
        state["aug"] = aug

    def gather_small():
        total = s_mid[...]
        for j in order:
            tiny_b[j].wait_recv()
            total = total + sd[j]
        s_near[...] = total

    def sums():
        tiny_c.wait_recv()
        total = s_near[...] + sx[...]
        state["denom"] = 1.0 + total[:, TILES:TILES + 1]
        state["total"] = total

    def make_reference(s, numer):
        total = state["total"]
        col = lax.broadcasted_iota(jnp.int32, (pr, pc), 1) + s * pc
        if subs > 1:
            col = col + lax.rem(core * near + slot, subs) * pcc
        scale = jnp.broadcast_to(total[:1, 0:1], (pr, pc))
        for t in range(1, TILES):
            scale = jnp.where(
                col >= t * (width // TILES), jnp.broadcast_to(total[:1, t:t + 1], (pr, pc)), scale
            )
        return numer / jnp.broadcast_to(state["denom"][:1], (pr, pc)) * scale

    xn = 2.0 * (lax.broadcasted_iota(jnp.int32, (1, width), 1).astype(jnp.float32) + 0.5) / width - 1.0
    span = max(16, pr)

    def xn_of(c0):
        return 2.0 * ((lax.broadcasted_iota(jnp.int32, (1, pc), 1) + c0).astype(jnp.float32) + 0.5) / width - 1.0

    def yn_of(row):
        return 2.0 * ((lax.broadcasted_iota(jnp.int32, (span, 1), 0) + row).astype(jnp.float32) + 0.5) / height - 1.0

    def fold(value):
        total = value[0:8, 0:LANES]
        for r in range(0, value.shape[0], 8):
            for c in range(0, value.shape[1], LANES):
                if r or c:
                    total = total + value[r:r + 8, c:c + LANES]
        return total

    def patch(ref, s, r0, sub):
        rows = [ref[piece(s, r0 // pr + q, sub)] for q in range(span // pr)]
        return rows[0] if len(rows) == 1 else jnp.concatenate(rows, axis=0)

    acc = [jnp.zeros((8, LANES), jnp.float32) for _ in range(NBASIS + 3)]

    def project(s):
        for r0 in range(0, height, span):
            for sub in range(subs):
                c0 = columns(s, sub)
                part = patch(g1, s, r0, sub) * hits[r0:r0 + span, c0:c0 + pc]
                for k in range(NBASIS):
                    base = bases[k * height + r0:k * height + r0 + span, c0:c0 + pc].astype(jnp.float32)
                    acc[k] = acc[k] + fold(part * base)
                acc[NBASIS] = acc[NBASIS] + fold(part)
                acc[NBASIS + 1] = acc[NBASIS + 1] + fold(part * xn_of(c0))
                acc[NBASIS + 2] = acc[NBASIS + 2] + fold(part * yn_of(r0))

    def solve():
        rows = [jnp.sum(value, axis=0, keepdims=True) for value in acc]
        rows.append(jnp.zeros((1, LANES), jnp.float32))
        rhs = jnp.sum(jnp.concatenate(rows, axis=0), axis=1, keepdims=True)
        coef = jnp.sum(state["aug"] * rhs, axis=0, keepdims=True)
        coef_ref[...] = coef[:, 0:NBASIS + 3]
        state["coefs"] = [jnp.broadcast_to(coef[:, k:k + 1], (span, LANES)) for k in range(NBASIS + 3)]

    mask_one = jnp.broadcast_to(mask[0:1, :], (pr, LANES))

    def residual(s, side):
        coefs = state["coefs"]
        for r0 in range(0, half_rows, span):
            row = pl.multiple_of(side * half_rows + r0, span)
            yterm = coefs[NBASIS] + coefs[NBASIS + 2] * yn_of(row)
            for sub in range(subs):
                for lo in range(0, pc, LANES):
                    c0 = columns(s, sub) + lo
                    xn = 2.0 * ((lax.broadcasted_iota(jnp.int32, (1, LANES), 1) + c0).astype(jnp.float32) + 0.5) / width - 1.0
                    model = yterm + coefs[NBASIS + 1] * xn
                    for k in range(NBASIS):
                        model = model + coefs[k] * bases[
                            pl.ds(pl.multiple_of(k * height + row, span), span), c0:c0 + LANES
                        ].astype(jnp.float32)
                    for q in range(span // pr):
                        at = piece(s, row // pr + q, sub)
                        diff = mask_one * (model[q * pr:(q + 1) * pr, :] - g1[at, :, lo:lo + LANES])
                        diff_ref[pl.ds(pl.multiple_of(row + q * pr, pr), pr), c0:c0 + LANES] = diff
                        x2[at, :, lo:lo + LANES] = diff * diff

    def root(s, pooled):
        return 1.0 / jnp.sqrt(0.05 + pooled / count)

    loads[0].wait()
    for s in range(stripes):
        weigh(s, 1 - core)
    enter_mate()
    for s in range(stripes):
        one.swap(s)
    tiny_a = tiny.start(s_own, sa, mate)
    loads[2].wait()
    for s in range(stripes):
        weigh(s, core)
    spread()
    horizontal(0)

    @pl.when(chip < near)
    def _():
        horizontal(1)
        horizontal(2)
        for si in range(3):
            vertical(si)

    for s in range(stripes):
        one.merge(s)
    tiny_a.wait_recv()
    s_mid[...] = s_own[...] + sa[...]
    enter_chips()
    for s in range(stripes):
        one.scatter(s)
    tiny_b = {j: tiny.start(s_mid, sd.at[j], device(to(j), core)) for j in order}

    @pl.when(chip >= near)
    def _():
        horizontal(1)
        horizontal(2)
        for si in range(3):
            vertical(si)

    stamped()
    for s in range(stripes):
        one.cross(s)
    gather_small()
    tiny_c = tiny.start(s_near, sx, device(to(near), core))
    for k in range(NBASIS):
        pick(k)
    invert()
    sums()
    for s in range(stripes):
        one.settle(s, make_reference)
    for s in range(stripes):
        one.hand(s)
    for s in range(stripes):
        one.end(s)
        project(s)
    solve()
    for s in range(stripes):
        residual(s, 1 - core)
        two.swap(s)
    for s in range(stripes):
        residual(s, core)
        two.merge(s)
        two.scatter(s)
    for s in range(stripes):
        two.cross(s)
    for s in range(stripes):
        two.settle(s, root)
    for s in range(stripes):
        two.hand(s)
    for s in range(stripes):
        two.end(s)
        for gi in range(height // pr):
            for sub in range(subs):
                c0 = columns(s, sub)
                inv_ref[gi * pr:(gi + 1) * pr, c0:c0 + pc] = g2[piece(s, gi, sub)]
    for copy in pending:
        copy.wait_send()


def finish(diff_ref, inv_ref, coef_in, out_ref, coef_ref):
    out_ref[0] = diff_ref[...] * inv_ref[...]
    coef_ref[...] = coef_in[...]


def shards(images, variance, zero_point, block_mask, stamps, owners):
    _, height, width = images.shape
    count = lax.axis_size("epoch")
    chips = count // 2
    npix = stamps.shape[1]
    near = chips // 2
    pr = max(8, height // chips)
    pcc = width * height // (chips * pr)
    stripes = 1
    while stripes < 2 and pcc // (stripes * 2) % LANES == 0:
        stripes *= 2
    pc = pcc // stripes
    f32 = jnp.float32
    big = pltpu.VMEM((stripes * chips, pr, pc), f32)
    part = pltpu.VMEM((stripes * near, pr, pc), f32)
    far = pltpu.VMEM((stripes, pr, pc), f32)
    tile = pltpu.VMEM((8, LANES), f32)
    nsem = stripes * (2 + 2 * (near - 1) + 1 + near // 2 + 1)
    dma = pltpu.SemaphoreType.DMA
    vmem = pl.BlockSpec(memory_space=pltpu.VMEM)
    smem = pl.BlockSpec(memory_space=pltpu.SMEM)
    hbm = pl.BlockSpec(memory_space=pltpu.HBM)
    images, owners, stamps = [pltpu.with_memory_space_constraint(v, pltpu.HBM) for v in (images, owners, stamps)]
    diff, inv, coef = pl.pallas_call(
        functools.partial(kernel, count, height, width, stripes),
        out_shape=(
            jax.ShapeDtypeStruct((height, width), f32),
            jax.ShapeDtypeStruct((height, width), f32),
            jax.ShapeDtypeStruct((1, NBASIS + 3), f32),
        ),
        in_specs=[hbm, smem, smem, smem, hbm, hbm],
        out_specs=(vmem,) * 3,
        scratch_shapes=[
            big, big, big, big, part, part, part, part, far, far,
            tile, tile, tile, tile, pltpu.VMEM((near, 8, LANES), f32), tile,
            pltpu.VMEM((width // LANES * height, 3 * LANES), jnp.bfloat16),
            pltpu.VMEM((9, height, width), jnp.bfloat16),
            pltpu.VMEM((NBASIS * height, width), jnp.bfloat16),
            pltpu.VMEM((width, npix), jnp.bfloat16),
            pltpu.VMEM((LANES, npix), f32),
            pltpu.VMEM((height, width), f32),
            pltpu.VMEM(images.shape, f32),
            pltpu.SMEM(owners.shape, jnp.int32),
            pltpu.VMEM(stamps.shape, jnp.int32), dma((4,)),
            dma((nsem,)), dma((nsem,)), dma((nsem,)), dma((nsem,)), dma((near + 1,)), dma((near + 1,)),
            pltpu.SemaphoreType.REGULAR,
        ],
        compiler_params=pltpu.CompilerParams(
            collective_id=0, has_side_effects=True, vmem_limit_bytes=40 * 1024 * 1024
        ),
    )(images, variance, zero_point, block_mask, owners, stamps)
    return pl.pallas_call(
        finish,
        out_shape=(
            jax.ShapeDtypeStruct((1, height, width), f32),
            jax.ShapeDtypeStruct((1, NBASIS + 3), f32),
        ),
        in_specs=[vmem] * 3,
        out_specs=(vmem,) * 2,
        compiler_params=pltpu.CompilerParams(vmem_limit_bytes=8 * 1024 * 1024),
    )(diff, inv, coef)


def solution(mesh):
    in_specs = (
        P(("patch", "epoch"), None, None),
        P(("patch", "epoch")),
        P(("patch", "epoch")),
        P(("patch", "epoch"), None),
        P(("patch", "epoch"), None),
        P("patch"),
    )
    out_specs = (P(("patch", "epoch"), None, None), P(("patch", "epoch"), None))
    return jax.shard_map(shards, mesh=mesh, in_specs=in_specs, out_specs=out_specs, check_vma=False)
```

```python
import functools
import math

import jax
import jax.numpy as jnp
from jax import lax
from jax.experimental import pallas as pl
from jax.experimental.pallas import tpu as pltpu
from jax.sharding import PartitionSpec as P

TILES = 4
KHALF = 7
NBASIS = 12
LANES = 128

sigma_list = (0.75, 1.5, 3.0)
basis_pairs = ((0, 0), (2, 0), (0, 2), (1, 1))
MESH = pl.DeviceIdType.MESH


def tap_values(offset, sigma, degree):
    scaled = offset / sigma
    power = jnp.ones_like(scaled)
    for _ in range(degree):
        power = power * scaled
    value = jnp.exp(-0.5 * scaled * scaled) * power / (math.sqrt(2.0 * math.pi) * sigma)
    return jnp.where(jnp.abs(offset) <= KHALF, value, 0.0).astype(jnp.bfloat16)


def kernel(
    count, height, width, stripes,
    image_in, var_ref, zp_ref, mask_ref, owner_in, stamp_in,
    diff_ref, inv_ref, coef_ref,
    x1, x2, g1, g2, ra1, ra2, rd1, rd2, rx1, rx2,
    s_own, s_mid, s_near, sa, sd, sx,
    lhs, across, bases, onehot, design, hits,
    image_ref, owner_ref, stamp_ref, load,
    send1, recv1, send2, recv2, send3, recv3, told,
):
    chips = count // 2
    _, pr, pc = x1.shape
    subs = width // (pc * stripes)
    pcc = pc * stripes
    npix = stamp_ref.shape[1]
    half_rows = height // 2

    me = lax.axis_index("epoch")
    core = lax.rem(me, 2)
    chip = me // 2
    near = chips // 2

    def device(which, cc):
        return {"epoch": which * 2 + cc}

    def to(j):
        value, bit = chip, 1
        while bit <= j:
            if j & bit:
                value = value + bit * (1 - 2 * lax.rem(chip // bit, 2))
            bit *= 2
        return value

    order = list(range(near - 1, 0, -1))
    mate = device(chip, 1 - core)
    slot = lax.rem(chip, near)

    barrier = pltpu.get_barrier_semaphore()

    @pl.when(core == 1)
    def _():
        pl.semaphore_signal(barrier, inc=1, device_id=mate, device_id_type=MESH)

    for j in order + [near]:
        pl.semaphore_signal(barrier, inc=1, device_id=device(to(j), 1), device_id_type=MESH)

    def enter_mate():
        @pl.when(core == 0)
        def _():
            pl.semaphore_wait(barrier, 1)
            pl.semaphore_signal(told, inc=1, device_id=mate, device_id_type=MESH)

        @pl.when(core == 1)
        def _():
            pl.semaphore_wait(told, 1)

    def enter_chips():
        @pl.when(core == 1)
        def _():
            pl.semaphore_wait(barrier, 2 * near)
            pl.semaphore_signal(told, inc=1, device_id=mate, device_id_type=MESH)

        @pl.when(core == 0)
        def _():
            pl.semaphore_wait(told, 1)

    def half_of(side):
        return pl.ds(pl.multiple_of(side * half_rows, 8), half_rows)

    loads = [
        pltpu.make_async_copy(src, dst, load.at[i])
        for i, (src, dst) in enumerate((
            (image_in.at[0, half_of(1 - core)], image_ref.at[0, half_of(1 - core)]), (owner_in, owner_ref),
            (image_in.at[0, half_of(core)], image_ref.at[0, half_of(core)]), (stamp_in, stamp_ref),
        ))
    ]
    for copy in loads:
        copy.start()

    pending = []

    class Lane:
        def __init__(self, send, recv):
            self.send, self.recv, self.next = send, recv, 0

        def start(self, src, dst, device_id):
            copy = pltpu.make_async_remote_copy(
                src_ref=src, dst_ref=dst, send_sem=self.send.at[self.next], recv_sem=self.recv.at[self.next],
                device_id=device_id, device_id_type=MESH,
            )
            self.next += 1
            copy.start()
            pending.append(copy)
            return copy

    def first(s, side):
        return (s * 2 + side) * near

    class Reduce:
        def __init__(self, x, g, ra, rd, rx, lane):
            self.x, self.g, self.ra, self.rd, self.rx, self.lane = x, g, ra, rd, rx, lane
            self.at = {}

        def swap(self, s):
            self.at["a", s] = self.lane.start(
                self.x.at[pl.ds(first(s, 1 - core), near)], self.ra.at[pl.ds(s * near, near)], mate
            )

        def merge(self, s):
            self.at["a", s].wait_recv()
            for c in range(near):
                own = first(s, core) + c
                self.x[own] = self.x[own] + self.ra[s * near + c]

        def scatter(self, s):
            for j in order:
                self.at["b", s, j] = self.lane.start(
                    self.x.at[first(s, core) + lax.rem(to(j), near)], self.rd.at[s * near + j], device(to(j), core)
                )

        def cross(self, s):
            own = first(s, core) + slot
            total = self.x[own]
            for j in order[::-1]:
                self.at["b", s, j].wait_recv()
                total = total + self.rd[s * near + j]
            self.x[own] = total
            self.at["c", s] = self.lane.start(self.x.at[own], self.rx.at[s], device(to(near), core))

        def settle(self, s, final):
            own = first(s, core) + slot
            self.at["c", s].wait_recv()
            self.g[own] = final(s, self.x[own] + self.rx[s])
            for j in order:
                self.at["d", s, j] = self.lane.start(self.g.at[own], self.g.at[own], device(to(j), core))
            block = self.g.at[pl.ds(own, 1)]
            self.at["e", s, 0] = self.lane.start(block, block, mate)

        def hand(self, s):
            for j in range(1, near):
                self.at["d", s, j].wait_recv()
                if j % 2:
                    where = lax.rem(to(j), near)
                    start = where if j == 1 else where // 2 * 2
                    block = self.g.at[pl.ds(first(s, core) + start, 1 if j == 1 else 2)]
                    self.at["e", s, j] = self.lane.start(block, block, mate)

        def end(self, s):
            for j in [0] + list(range(1, near, 2)):
                self.at["e", s, j].wait_recv()

    def columns(s, sub):
        return sub * pcc + s * pc

    def piece(s, gi, sub):
        return 2 * near * s + gi * subs + sub

    one = Reduce(x1, g1, ra1, rd1, rx1, Lane(send1, recv1))
    two = Reduce(x2, g2, ra2, rd2, rx2, Lane(send2, recv2))
    tiny = Lane(send3, recv3)

    weight = 1.0 / jnp.full((8, LANES), var_ref[0], jnp.float32)
    mask = jnp.full((8, LANES), mask_ref[0, 0].astype(jnp.float32), jnp.float32)
    block_term = weight * mask
    term = block_term[0:1, 0:1]
    lane = lax.broadcasted_iota(jnp.int32, (8, LANES), 1)
    loads[1].wait()
    small = jnp.where(lane == TILES, block_term, 0.0)
    for t in range(TILES):
        value = jnp.where(owner_ref[t] == me, zp_ref[0], 0.0)
        small = small + jnp.where(lane == t, value, 0.0)
    s_own[...] = small

    def weigh(s, side):
        for r0 in range(0, half_rows, pr):
            row = pl.multiple_of(side * half_rows + r0, pr)
            for sub in range(subs):
                c0 = columns(s, sub)
                x1[piece(s, row // pr, sub)] = image_ref[0, pl.ds(row, pr), c0:c0 + pc] * term

    ntile = width // LANES
    zero = jnp.zeros((height, LANES), jnp.bfloat16)

    def spread():
        sharp = image_ref[0].astype(jnp.bfloat16)
        for t in range(ntile):
            for s in range(3):
                src = t + s - 1
                value = sharp[:, src * LANES:(src + 1) * LANES] if 0 <= src < ntile else zero
                lhs[t * height:(t + 1) * height, s * LANES:(s + 1) * LANES] = value

    off_h = (
        lax.broadcasted_iota(jnp.int32, (3 * LANES, LANES), 0)
        - LANES
        - lax.broadcasted_iota(jnp.int32, (3 * LANES, LANES), 1)
    ).astype(jnp.float32)
    off_v = (
        lax.broadcasted_iota(jnp.int32, (height, height), 1) - lax.broadcasted_iota(jnp.int32, (height, height), 0)
    ).astype(jnp.float32)

    def horizontal(si):
        sigma = sigma_list[si]
        band = jnp.concatenate([tap_values(off_h, sigma, degree) for degree in (0, 1, 2)], axis=1)
        for t in range(0, ntile, 2):
            res = jnp.dot(
                lhs[t * height:(t + 2) * height, :], band, preferred_element_type=jnp.float32
            ).astype(jnp.bfloat16)
            for u in range(2):
                for degree in (0, 1, 2):
                    across[si * 3 + degree, :, (t + u) * LANES:(t + u + 1) * LANES] = res[
                        u * height:(u + 1) * height, degree * LANES:(degree + 1) * LANES
                    ]

    def vertical(si):
        sigma = sigma_list[si]
        bands = [tap_values(off_v, sigma, degree) for degree in (0, 1, 2)]
        for i, j in basis_pairs:
            k = si * 4 + basis_pairs.index((i, j))
            bases[k * height:(k + 1) * height, :] = jnp.dot(
                bands[j], across[si * 3 + i], preferred_element_type=jnp.float32
            ).astype(jnp.bfloat16)

    state = {}

    def stamped():
        loads[3].wait()
        stamp = stamp_ref[...]
        shift = width.bit_length() - 1
        rows = lax.shift_right_logical(stamp, shift)
        cols = stamp - lax.shift_left(rows, shift)
        onehot[...] = jnp.where(
            lax.broadcasted_iota(jnp.int32, (width, npix), 0) == cols, 1.0, 0.0
        ).astype(jnp.bfloat16)
        row_hit = lax.broadcasted_iota(jnp.int32, (height, npix), 0) == rows
        state["hit"] = row_hit
        hits[...] = lax.dot_general(
            jnp.where(row_hit, 1.0, 0.0).astype(jnp.bfloat16), onehot[...], (((1,), (1,)), ((), ())),
            preferred_element_type=jnp.float32,
        )
        design[...] = jnp.zeros_like(design)
        design[16 + NBASIS:17 + NBASIS, :] = jnp.ones((1, npix), jnp.float32)
        design[17 + NBASIS:18 + NBASIS, :] = 2.0 * (cols.astype(jnp.float32) + 0.5) / width - 1.0
        design[18 + NBASIS:19 + NBASIS, :] = 2.0 * (rows.astype(jnp.float32) + 0.5) / height - 1.0

    def pick(k):
        got = jnp.dot(
            bases[k * height:(k + 1) * height, :], onehot[...], preferred_element_type=jnp.float32
        )
        design[16 + k:17 + k, :] = jnp.sum(jnp.where(state["hit"], got, 0.0), axis=0, keepdims=True)

    def invert():
        rowi = lax.broadcasted_iota(jnp.int32, (16, LANES), 0)
        lanei = lax.broadcasted_iota(jnp.int32, (16, LANES), 1)
        normal = lax.dot_general(
            design[16:32, :], design[...], (((1,), (1,)), ((), ())),
            precision=lax.Precision.HIGHEST, preferred_element_type=jnp.float32,
        )
        aug = jnp.where(lanei == rowi + 16, normal + 0.05 * normal, normal)
        aug = jnp.where(lanei == rowi, 1.0, aug)
        aug = jnp.where((rowi == 15) & (lanei == 31), 1.0, aug)
        for k in range(NBASIS + 3):
            row = aug[k:k + 1, :] / aug[k:k + 1, 16 + k:17 + k]
            aug = jnp.where(rowi == k, row, aug - aug[:, 16 + k:17 + k] * row)
        state["aug"] = aug

    def gather_small():
        total = s_mid[...]
        for j in order:
            tiny_b[j].wait_recv()
            total = total + sd[j]
        s_near[...] = total

    def sums():
        tiny_c.wait_recv()
        total = s_near[...] + sx[...]
        state["denom"] = 1.0 + total[:, TILES:TILES + 1]
        state["total"] = total

    def make_reference(s, numer):
        total = state["total"]
        col = lax.broadcasted_iota(jnp.int32, (pr, pc), 1) + s * pc
        if subs > 1:
            col = col + lax.rem(core * near + slot, subs) * pcc
        scale = jnp.broadcast_to(total[:1, 0:1], (pr, pc))
        for t in range(1, TILES):
            scale = jnp.where(
                col >= t * (width // TILES), jnp.broadcast_to(total[:1, t:t + 1], (pr, pc)), scale
            )
        return numer / jnp.broadcast_to(state["denom"][:1], (pr, pc)) * scale

    span = max(16, pr)

    def xn_of(c0):
        return 2.0 * ((lax.broadcasted_iota(jnp.int32, (1, pc), 1) + c0).astype(jnp.float32) + 0.5) / width - 1.0

    def yn_of(row):
        return 2.0 * ((lax.broadcasted_iota(jnp.int32, (span, 1), 0) + row).astype(jnp.float32) + 0.5) / height - 1.0

    def fold(value):
        total = value[0:8, 0:LANES]
        for r in range(0, value.shape[0], 8):
            for c in range(0, value.shape[1], LANES):
                if r or c:
                    total = total + value[r:r + 8, c:c + LANES]
        return total

    def patch(ref, s, r0, sub):
        rows = [ref[piece(s, r0 // pr + q, sub)] for q in range(span // pr)]
        return rows[0] if len(rows) == 1 else jnp.concatenate(rows, axis=0)

    acc = [jnp.zeros((8, LANES), jnp.float32) for _ in range(NBASIS + 3)]

    def project(s):
        for r0 in range(0, height, span):
            for sub in range(subs):
                c0 = columns(s, sub)
                part = patch(g1, s, r0, sub) * hits[r0:r0 + span, c0:c0 + pc]
                for k in range(NBASIS):
                    base = bases[k * height + r0:k * height + r0 + span, c0:c0 + pc].astype(jnp.float32)
                    acc[k] = acc[k] + fold(part * base)
                acc[NBASIS] = acc[NBASIS] + fold(part)
                acc[NBASIS + 1] = acc[NBASIS + 1] + fold(part * xn_of(c0))
                acc[NBASIS + 2] = acc[NBASIS + 2] + fold(part * yn_of(r0))

    def solve():
        rows = [jnp.sum(value, axis=0, keepdims=True) for value in acc]
        rows.append(jnp.zeros((1, LANES), jnp.float32))
        rhs = jnp.sum(jnp.concatenate(rows, axis=0), axis=1, keepdims=True)
        coef = jnp.sum(state["aug"] * rhs, axis=0, keepdims=True)
        coef_ref[...] = coef[:, 0:NBASIS + 3]
        state["coefs"] = [jnp.broadcast_to(coef[:, k:k + 1], (span, LANES)) for k in range(NBASIS + 3)]

    mask_one = jnp.broadcast_to(mask[0:1, :], (pr, LANES))

    def residual(s, side):
        coefs = state["coefs"]
        for r0 in range(0, half_rows, span):
            row = pl.multiple_of(side * half_rows + r0, span)
            yterm = coefs[NBASIS] + coefs[NBASIS + 2] * yn_of(row)
            for sub in range(subs):
                for lo in range(0, pc, LANES):
                    c0 = columns(s, sub) + lo
                    xn = 2.0 * ((lax.broadcasted_iota(jnp.int32, (1, LANES), 1) + c0).astype(jnp.float32) + 0.5) / width - 1.0
                    model = yterm + coefs[NBASIS + 1] * xn
                    for k in range(NBASIS):
                        model = model + coefs[k] * bases[
                            pl.ds(pl.multiple_of(k * height + row, span), span), c0:c0 + LANES
                        ].astype(jnp.float32)
                    for q in range(span // pr):
                        at = piece(s, row // pr + q, sub)
                        diff = mask_one * (model[q * pr:(q + 1) * pr, :] - g1[at, :, lo:lo + LANES])
                        diff_ref[pl.ds(pl.multiple_of(row + q * pr, pr), pr), c0:c0 + LANES] = diff
                        x2[at, :, lo:lo + LANES] = diff * diff

    def root(s, pooled):
        return 1.0 / jnp.sqrt(0.05 + pooled / count)

    loads[0].wait()
    for s in range(stripes):
        weigh(s, 1 - core)
    enter_mate()
    for s in range(stripes):
        one.swap(s)
    tiny_a = tiny.start(s_own, sa, mate)
    loads[2].wait()
    for s in range(stripes):
        weigh(s, core)
    spread()
    horizontal(0)

    @pl.when(chip < near // 2)
    def _():
        horizontal(1)
        horizontal(2)
        for si in range(3):
            vertical(si)

    for s in range(stripes):
        one.merge(s)
    tiny_a.wait_recv()
    s_mid[...] = s_own[...] + sa[...]
    enter_chips()
    for s in range(stripes):
        one.scatter(s)
    tiny_b = {j: tiny.start(s_mid, sd.at[j], device(to(j), core)) for j in order}

    @pl.when(chip >= near // 2)
    def _():
        horizontal(1)
        horizontal(2)
        for si in range(3):
            vertical(si)

    stamped()
    for k in range(NBASIS):
        pick(k)
    for s in range(stripes):
        one.cross(s)
    gather_small()
    tiny_c = tiny.start(s_near, sx, device(to(near), core))
    invert()
    sums()
    for s in range(stripes):
        one.settle(s, make_reference)
    for s in range(stripes):
        one.hand(s)
    for s in range(stripes):
        one.end(s)
        project(s)
    solve()
    for s in range(stripes):
        residual(s, 1 - core)
        two.swap(s)
    for s in range(stripes):
        residual(s, core)
        two.merge(s)
        two.scatter(s)
    for s in range(stripes):
        two.cross(s)
    for s in range(stripes):
        two.settle(s, root)
    for s in range(stripes):
        two.hand(s)
    for s in range(stripes):
        two.end(s)
        for gi in range(height // pr):
            for sub in range(subs):
                c0 = columns(s, sub)
                inv_ref[gi * pr:(gi + 1) * pr, c0:c0 + pc] = g2[piece(s, gi, sub)]
    for copy in pending:
        copy.wait_send()


def finish(diff_ref, inv_ref, coef_in, out_ref, coef_ref):
    out_ref[0] = diff_ref[...] * inv_ref[...]
    coef_ref[...] = coef_in[...]


def shards(images, variance, zero_point, block_mask, stamps, owners):
    _, height, width = images.shape
    count = lax.axis_size("epoch")
    chips = count // 2
    npix = stamps.shape[1]
    near = chips // 2
    pr = max(8, height // chips)
    pcc = width * height // (chips * pr)
    stripes = 1
    while stripes < 2 and pcc // (stripes * 2) % LANES == 0:
        stripes *= 2
    pc = pcc // stripes
    f32 = jnp.float32
    big = pltpu.VMEM((stripes * chips, pr, pc), f32)
    part = pltpu.VMEM((stripes * near, pr, pc), f32)
    far = pltpu.VMEM((stripes, pr, pc), f32)
    tile = pltpu.VMEM((8, LANES), f32)
    nsem = stripes * (2 + 2 * (near - 1) + 1 + near // 2 + 1)
    dma = pltpu.SemaphoreType.DMA
    vmem = pl.BlockSpec(memory_space=pltpu.VMEM)
    smem = pl.BlockSpec(memory_space=pltpu.SMEM)
    hbm = pl.BlockSpec(memory_space=pltpu.HBM)
    images, owners, stamps = [pltpu.with_memory_space_constraint(v, pltpu.HBM) for v in (images, owners, stamps)]
    diff, inv, coef = pl.pallas_call(
        functools.partial(kernel, count, height, width, stripes),
        out_shape=(
            jax.ShapeDtypeStruct((height, width), f32),
            jax.ShapeDtypeStruct((height, width), f32),
            jax.ShapeDtypeStruct((1, NBASIS + 3), f32),
        ),
        in_specs=[hbm, smem, smem, smem, hbm, hbm],
        out_specs=(vmem,) * 3,
        scratch_shapes=[
            big, big, big, big, part, part, part, part, far, far,
            tile, tile, tile, tile, pltpu.VMEM((near, 8, LANES), f32), tile,
            pltpu.VMEM((width // LANES * height, 3 * LANES), jnp.bfloat16),
            pltpu.VMEM((9, height, width), jnp.bfloat16),
            pltpu.VMEM((NBASIS * height, width), jnp.bfloat16),
            pltpu.VMEM((width, npix), jnp.bfloat16),
            pltpu.VMEM((LANES, npix), f32),
            pltpu.VMEM((height, width), f32),
            pltpu.VMEM(images.shape, f32),
            pltpu.SMEM(owners.shape, jnp.int32),
            pltpu.VMEM(stamps.shape, jnp.int32), dma((4,)),
            dma((nsem,)), dma((nsem,)), dma((nsem,)), dma((nsem,)), dma((near + 1,)), dma((near + 1,)),
            pltpu.SemaphoreType.REGULAR,
        ],
        compiler_params=pltpu.CompilerParams(
            collective_id=0, has_side_effects=True, vmem_limit_bytes=40 * 1024 * 1024
        ),
    )(images, variance, zero_point, block_mask, owners, stamps)
    return pl.pallas_call(
        finish,
        out_shape=(
            jax.ShapeDtypeStruct((1, height, width), f32),
            jax.ShapeDtypeStruct((1, NBASIS + 3), f32),
        ),
        in_specs=[vmem] * 3,
        out_specs=(vmem,) * 2,
        compiler_params=pltpu.CompilerParams(vmem_limit_bytes=8 * 1024 * 1024),
    )(diff, inv, coef)


def solution(mesh):
    in_specs = (
        P(("patch", "epoch"), None, None),
        P(("patch", "epoch")),
        P(("patch", "epoch")),
        P(("patch", "epoch"), None),
        P(("patch", "epoch"), None),
        P("patch"),
    )
    out_specs = (P(("patch", "epoch"), None, None), P(("patch", "epoch"), None))
    return jax.shard_map(shards, mesh=mesh, in_specs=in_specs, out_specs=out_specs, check_vma=False)
```

```python
import functools
import math

import jax
import jax.numpy as jnp
from jax import lax
from jax.experimental import pallas as pl
from jax.experimental.pallas import tpu as pltpu
from jax.sharding import PartitionSpec as P

TILES = 4
KHALF = 7
NBASIS = 12
LANES = 128

sigma_list = (0.75, 1.5, 3.0)
basis_pairs = ((0, 0), (2, 0), (0, 2), (1, 1))
MESH = pl.DeviceIdType.MESH


def tap_values(offset, sigma, degree):
    scaled = offset / sigma
    power = jnp.ones_like(scaled)
    for _ in range(degree):
        power = power * scaled
    value = jnp.exp(-0.5 * scaled * scaled) * power / (math.sqrt(2.0 * math.pi) * sigma)
    return jnp.where(jnp.abs(offset) <= KHALF, value, 0.0).astype(jnp.bfloat16)


def kernel(
    count, height, width, stripes,
    image_in, var_ref, zp_ref, mask_ref, owner_in, stamp_in,
    diff_ref, coef_ref,
    x1, x2, g1, g2, ra1, ra2, rd1, rd2, rx1, rx2,
    s_own, s_mid, s_near, sa, sd, sx,
    lhs, across, bases, wide, onehot, design, hits,
    image_ref, owner_ref, stamp_ref, load,
    send1, recv1, send2, recv2, send3, recv3, told,
):
    chips = count // 2
    _, pr, pc = x1.shape
    subs = width // (pc * stripes)
    pcc = pc * stripes
    npix = stamp_ref.shape[1]
    half_rows = height // 2

    me = lax.axis_index("epoch")
    core = lax.rem(me, 2)
    chip = me // 2
    near = chips // 2

    def device(which, cc):
        return {"epoch": which * 2 + cc}

    def to(j):
        value, bit = chip, 1
        while bit <= j:
            if j & bit:
                value = value + bit * (1 - 2 * lax.rem(chip // bit, 2))
            bit *= 2
        return value

    order = list(range(near - 1, 0, -1))
    mate = device(chip, 1 - core)
    slot = lax.rem(chip, near)

    barrier = pltpu.get_barrier_semaphore()

    @pl.when(core == 1)
    def _():
        pl.semaphore_signal(barrier, inc=1, device_id=mate, device_id_type=MESH)

    for j in order + [near]:
        pl.semaphore_signal(barrier, inc=1, device_id=device(to(j), 1), device_id_type=MESH)

    def enter_mate():
        @pl.when(core == 0)
        def _():
            pl.semaphore_wait(barrier, 1)
            pl.semaphore_signal(told, inc=1, device_id=mate, device_id_type=MESH)

        @pl.when(core == 1)
        def _():
            pl.semaphore_wait(told, 1)

    def enter_chips():
        @pl.when(core == 1)
        def _():
            pl.semaphore_wait(barrier, 2 * near)
            pl.semaphore_signal(told, inc=1, device_id=mate, device_id_type=MESH)

        @pl.when(core == 0)
        def _():
            pl.semaphore_wait(told, 1)

    def half_of(side, part=0):
        return pl.ds(pl.multiple_of(side * half_rows + part * (half_rows // 2), 8), half_rows // 2)

    loads = [
        pltpu.make_async_copy(src, dst, load.at[i])
        for i, (src, dst) in enumerate((
            (image_in.at[0, half_of(1 - core)], image_ref.at[0, half_of(1 - core)]), (owner_in, owner_ref),
            (image_in.at[0, half_of(core)], image_ref.at[0, half_of(core)]), (stamp_in, stamp_ref),
            (image_in.at[0, half_of(1 - core, 1)], image_ref.at[0, half_of(1 - core, 1)]),
            (image_in.at[0, half_of(core, 1)], image_ref.at[0, half_of(core, 1)]),
        ))
    ]
    for copy in loads:
        copy.start()

    pending = []

    class Lane:
        def __init__(self, send, recv):
            self.send, self.recv, self.next = send, recv, 0

        def start(self, src, dst, device_id):
            copy = pltpu.make_async_remote_copy(
                src_ref=src, dst_ref=dst, send_sem=self.send.at[self.next], recv_sem=self.recv.at[self.next],
                device_id=device_id, device_id_type=MESH,
            )
            self.next += 1
            copy.start()
            pending.append(copy)
            return copy

    def first(s, side):
        return (s * 2 + side) * near

    class Reduce:
        def __init__(self, x, g, ra, rd, rx, lane):
            self.x, self.g, self.ra, self.rd, self.rx, self.lane = x, g, ra, rd, rx, lane
            self.at = {}

        def swap(self, s):
            self.at["a", s] = self.lane.start(
                self.x.at[pl.ds(first(s, 1 - core), near)], self.ra.at[pl.ds(s * near, near)], mate
            )

        def merge(self, s):
            self.at["a", s].wait_recv()
            for c in range(near):
                own = first(s, core) + c
                self.x[own] = self.x[own] + self.ra[s * near + c]

        def scatter(self, s):
            for j in order:
                self.at["b", s, j] = self.lane.start(
                    self.x.at[first(s, core) + lax.rem(to(j), near)], self.rd.at[s * near + j], device(to(j), core)
                )

        def cross(self, s):
            own = first(s, core) + slot
            total = self.x[own]
            for j in order[::-1]:
                self.at["b", s, j].wait_recv()
                total = total + self.rd[s * near + j]
            self.x[own] = total
            self.at["c", s] = self.lane.start(self.x.at[own], self.rx.at[s], device(to(near), core))

        def settle(self, s, final):
            own = first(s, core) + slot
            self.at["c", s].wait_recv()
            self.g[own] = final(s, self.x[own] + self.rx[s])
            for j in order:
                self.at["d", s, j] = self.lane.start(self.g.at[own], self.g.at[own], device(to(j), core))
            block = self.g.at[pl.ds(own, 1)]
            self.at["e", s, 0] = self.lane.start(block, block, mate)

        def hand(self, s):
            for j in range(1, near):
                self.at["d", s, j].wait_recv()
                if j % 2:
                    where = lax.rem(to(j), near)
                    start = where if j == 1 else where // 2 * 2
                    block = self.g.at[pl.ds(first(s, core) + start, 1 if j == 1 else 2)]
                    self.at["e", s, j] = self.lane.start(block, block, mate)

        def end(self, s):
            for j in [0] + list(range(1, near, 2)):
                self.at["e", s, j].wait_recv()

    def columns(s, sub):
        return sub * pcc + s * pc

    def piece(s, gi, sub):
        return 2 * near * s + gi * subs + sub

    one = Reduce(x1, g1, ra1, rd1, rx1, Lane(send1, recv1))
    two = Reduce(x2, g2, ra2, rd2, rx2, Lane(send2, recv2))
    tiny = Lane(send3, recv3)

    weight = 1.0 / jnp.full((8, LANES), var_ref[0], jnp.float32)
    mask = jnp.full((8, LANES), mask_ref[0, 0].astype(jnp.float32), jnp.float32)
    block_term = weight * mask
    term = block_term[0:1, 0:1]
    lane = lax.broadcasted_iota(jnp.int32, (8, LANES), 1)
    loads[1].wait()
    small = jnp.where(lane == TILES, block_term, 0.0)
    for t in range(TILES):
        value = jnp.where(owner_ref[t] == me, zp_ref[0], 0.0)
        small = small + jnp.where(lane == t, value, 0.0)
    s_own[...] = small

    def weigh(s, side):
        for r0 in range(0, half_rows, pr):
            row = pl.multiple_of(side * half_rows + r0, pr)
            for sub in range(subs):
                c0 = columns(s, sub)
                x1[piece(s, row // pr, sub)] = image_ref[0, pl.ds(row, pr), c0:c0 + pc] * term

    ntile = width // LANES
    zero = jnp.zeros((height, LANES), jnp.bfloat16)

    def spread():
        sharp = image_ref[0].astype(jnp.bfloat16)
        for t in range(ntile):
            for s in range(3):
                src = t + s - 1
                value = sharp[:, src * LANES:(src + 1) * LANES] if 0 <= src < ntile else zero
                lhs[t * height:(t + 1) * height, s * LANES:(s + 1) * LANES] = value

    off_h = (
        lax.broadcasted_iota(jnp.int32, (3 * LANES, LANES), 0)
        - LANES
        - lax.broadcasted_iota(jnp.int32, (3 * LANES, LANES), 1)
    ).astype(jnp.float32)
    off_v = (
        lax.broadcasted_iota(jnp.int32, (height, height), 1) - lax.broadcasted_iota(jnp.int32, (height, height), 0)
    ).astype(jnp.float32)

    def horizontal(si):
        sigma = sigma_list[si]
        band = jnp.concatenate([tap_values(off_h, sigma, degree) for degree in (0, 1, 2)], axis=1)
        for t in range(0, ntile, 2):
            res = jnp.dot(
                lhs[t * height:(t + 2) * height, :], band, preferred_element_type=jnp.float32
            ).astype(jnp.bfloat16)
            for u in range(2):
                for degree in (0, 1, 2):
                    across[si * 3 + degree, :, (t + u) * LANES:(t + u + 1) * LANES] = res[
                        u * height:(u + 1) * height, degree * LANES:(degree + 1) * LANES
                    ]

    def vertical(si):
        sigma = sigma_list[si]
        bands = [tap_values(off_v, sigma, degree) for degree in (0, 1, 2)]
        for i, j in basis_pairs:
            k = si * 4 + basis_pairs.index((i, j))
            bases[k * height:(k + 1) * height, :] = jnp.dot(
                bands[j], across[si * 3 + i], preferred_element_type=jnp.float32
            ).astype(jnp.bfloat16)

    state = {}

    def stamped():
        loads[3].wait()
        stamp = stamp_ref[...]
        shift = width.bit_length() - 1
        rows = lax.shift_right_logical(stamp, shift)
        cols = stamp - lax.shift_left(rows, shift)
        onehot[...] = jnp.where(
            lax.broadcasted_iota(jnp.int32, (width, npix), 0) == cols, 1.0, 0.0
        ).astype(jnp.bfloat16)
        row_hit = lax.broadcasted_iota(jnp.int32, (height, npix), 0) == rows
        state["hit"] = row_hit
        hits[...] = lax.dot_general(
            jnp.where(row_hit, 1.0, 0.0).astype(jnp.bfloat16), onehot[...], (((1,), (1,)), ((), ())),
            preferred_element_type=jnp.float32,
        )
        design[...] = jnp.zeros_like(design)
        design[16 + NBASIS:17 + NBASIS, :] = jnp.ones((1, npix), jnp.float32)
        design[17 + NBASIS:18 + NBASIS, :] = 2.0 * (cols.astype(jnp.float32) + 0.5) / width - 1.0
        design[18 + NBASIS:19 + NBASIS, :] = 2.0 * (rows.astype(jnp.float32) + 0.5) / height - 1.0

    def pick(k):
        got = jnp.dot(
            bases[k * height:(k + 1) * height, :], onehot[...], preferred_element_type=jnp.float32
        )
        design[16 + k:17 + k, :] = jnp.sum(jnp.where(state["hit"], got, 0.0), axis=0, keepdims=True)

    def invert():
        rowi = lax.broadcasted_iota(jnp.int32, (16, LANES), 0)
        lanei = lax.broadcasted_iota(jnp.int32, (16, LANES), 1)
        normal = lax.dot_general(
            design[16:32, :], design[...], (((1,), (1,)), ((), ())),
            precision=lax.Precision.HIGHEST, preferred_element_type=jnp.float32,
        )
        aug = jnp.where(lanei == rowi + 16, normal + 0.05 * normal, normal)
        aug = jnp.where(lanei == rowi, 1.0, aug)
        aug = jnp.where((rowi == 15) & (lanei == 31), 1.0, aug)
        for k in range(NBASIS + 3):
            row = aug[k:k + 1, :] / aug[k:k + 1, 16 + k:17 + k]
            aug = jnp.where(rowi == k, row, aug - aug[:, 16 + k:17 + k] * row)
        state["aug"] = aug

    def gather_small():
        total = s_mid[...]
        for j in order:
            tiny_b[j].wait_recv()
            total = total + sd[j]
        s_near[...] = total

    def sums():
        tiny_c.wait_recv()
        total = s_near[...] + sx[...]
        state["denom"] = 1.0 + total[:, TILES:TILES + 1]
        state["total"] = total

    def make_reference(s, numer):
        total = state["total"]
        col = lax.broadcasted_iota(jnp.int32, (pr, pc), 1) + s * pc
        if subs > 1:
            col = col + lax.rem(core * near + slot, subs) * pcc
        scale = jnp.broadcast_to(total[:1, 0:1], (pr, pc))
        for t in range(1, TILES):
            scale = jnp.where(
                col >= t * (width // TILES), jnp.broadcast_to(total[:1, t:t + 1], (pr, pc)), scale
            )
        return numer / jnp.broadcast_to(state["denom"][:1], (pr, pc)) * scale

    xn = 2.0 * (lax.broadcasted_iota(jnp.int32, (1, width), 1).astype(jnp.float32) + 0.5) / width - 1.0
    span = max(16, pr)

    def xn_of(c0):
        return 2.0 * ((lax.broadcasted_iota(jnp.int32, (1, pc), 1) + c0).astype(jnp.float32) + 0.5) / width - 1.0

    def yn_of(row):
        return 2.0 * ((lax.broadcasted_iota(jnp.int32, (span, 1), 0) + row).astype(jnp.float32) + 0.5) / height - 1.0

    def fold(value):
        total = value[0:8, 0:LANES]
        for r in range(0, value.shape[0], 8):
            for c in range(0, value.shape[1], LANES):
                if r or c:
                    total = total + value[r:r + 8, c:c + LANES]
        return total

    def patch(ref, s, r0, sub):
        rows = [ref[piece(s, r0 // pr + q, sub)] for q in range(span // pr)]
        return rows[0] if len(rows) == 1 else jnp.concatenate(rows, axis=0)

    acc = [jnp.zeros((8, LANES), jnp.float32) for _ in range(NBASIS + 3)]

    def project(s):
        for r0 in range(0, height, span):
            for sub in range(subs):
                c0 = columns(s, sub)
                part = patch(g1, s, r0, sub) * hits[r0:r0 + span, c0:c0 + pc]
                for k in range(NBASIS):
                    base = wide[k * height + r0:k * height + r0 + span, c0:c0 + pc]
                    acc[k] = acc[k] + fold(part * base)
                acc[NBASIS] = acc[NBASIS] + fold(part)
                acc[NBASIS + 1] = acc[NBASIS + 1] + fold(part * xn_of(c0))
                acc[NBASIS + 2] = acc[NBASIS + 2] + fold(part * yn_of(r0))

    def solve():
        rows = [jnp.sum(value, axis=0, keepdims=True) for value in acc]
        rows.append(jnp.zeros((1, LANES), jnp.float32))
        rhs = jnp.sum(jnp.concatenate(rows, axis=0), axis=1, keepdims=True)
        coef = jnp.sum(state["aug"] * rhs, axis=0, keepdims=True)
        coef_ref[...] = coef[:, 0:NBASIS + 3]
        state["coefs"] = [jnp.broadcast_to(coef[:, k:k + 1], (span, LANES)) for k in range(NBASIS + 3)]

    mask_one = jnp.broadcast_to(mask[0:1, :], (pr, LANES))

    def residual(s, side):
        coefs = state["coefs"]
        for r0 in range(0, half_rows, span):
            row = pl.multiple_of(side * half_rows + r0, span)
            yterm = coefs[NBASIS] + coefs[NBASIS + 2] * yn_of(row)
            for sub in range(subs):
                for lo in range(0, pc, LANES):
                    c0 = columns(s, sub) + lo
                    xn = 2.0 * ((lax.broadcasted_iota(jnp.int32, (1, LANES), 1) + c0).astype(jnp.float32) + 0.5) / width - 1.0
                    model = yterm + coefs[NBASIS + 1] * xn
                    for k in range(NBASIS):
                        model = model + coefs[k] * wide[
                            pl.ds(pl.multiple_of(k * height + row, span), span), c0:c0 + LANES
                        ]
                    for q in range(span // pr):
                        at = piece(s, row // pr + q, sub)
                        diff = mask_one * (model[q * pr:(q + 1) * pr, :] - g1[at, :, lo:lo + LANES])
                        diff_ref[pl.ds(pl.multiple_of(row + q * pr, pr), pr), c0:c0 + LANES] = diff
                        x2[at, :, lo:lo + LANES] = diff * diff

    def root(s, pooled):
        return 1.0 / jnp.sqrt(0.05 + pooled / count)

    loads[0].wait()
    loads[4].wait()
    for s in range(stripes):
        weigh(s, 1 - core)
    enter_mate()
    for s in range(stripes):
        one.swap(s)
    tiny_a = tiny.start(s_own, sa, mate)
    loads[2].wait()
    loads[5].wait()
    for s in range(stripes):
        weigh(s, core)
    spread()
    horizontal(0)

    @pl.when(chip < near // 2)
    def _():
        horizontal(1)
        horizontal(2)
        for si in range(3):
            vertical(si)

    for s in range(stripes):
        one.merge(s)
    tiny_a.wait_recv()
    s_mid[...] = s_own[...] + sa[...]
    enter_chips()
    for s in range(stripes):
        one.scatter(s)
    tiny_b = {j: tiny.start(s_mid, sd.at[j], device(to(j), core)) for j in order}

    @pl.when(chip >= near // 2)
    def _():
        horizontal(1)
        horizontal(2)
        for si in range(3):
            vertical(si)

    stamped()
    for k in range(NBASIS):
        pick(k)
    for s in range(stripes):
        one.cross(s)
    gather_small()
    tiny_c = tiny.start(s_near, sx, device(to(near), core))
    invert()
    for k in range(NBASIS):
        wide[k * height:(k + 1) * height, :] = bases[k * height:(k + 1) * height, :].astype(jnp.float32)
    sums()
    for s in range(stripes):
        one.settle(s, make_reference)
    for s in range(stripes):
        one.hand(s)
    for s in range(stripes):
        one.end(s)
        project(s)
    solve()
    for s in range(stripes):
        residual(s, 1 - core)
        two.swap(s)
    for s in range(stripes):
        residual(s, core)
        two.merge(s)
        two.scatter(s)
    for s in range(stripes):
        two.cross(s)
    for s in range(stripes):
        two.settle(s, root)
    for s in range(stripes):
        two.hand(s)
    for s in range(stripes):
        two.end(s)
        for gi in range(height // pr):
            for sub in range(subs):
                c0 = columns(s, sub)
                spot = (slice(gi * pr, (gi + 1) * pr), slice(c0, c0 + pc))
                diff_ref[spot] = diff_ref[spot] * g2[piece(s, gi, sub)]
    for copy in pending:
        copy.wait_send()


def finish(value_ref, coef_in, out_ref, coef_ref, sem):
    parts = sem.shape[0] - 1
    rows = value_ref.shape[0] // parts
    copies = [pltpu.make_async_copy(coef_in, coef_ref, sem.at[parts])]
    for i in range(parts):
        spot = pl.ds(i * rows, rows)
        copies.append(pltpu.make_async_copy(value_ref.at[spot], out_ref.at[0, spot], sem.at[i]))
    for copy in copies:
        copy.start()
    for copy in copies:
        copy.wait()


def shards(images, variance, zero_point, block_mask, stamps, owners):
    _, height, width = images.shape
    count = lax.axis_size("epoch")
    chips = count // 2
    npix = stamps.shape[1]
    near = chips // 2
    pr = max(8, height // chips)
    pcc = width * height // (chips * pr)
    stripes = 1
    while stripes < 2 and pcc // (stripes * 2) % LANES == 0:
        stripes *= 2
    pc = pcc // stripes
    f32 = jnp.float32
    big = pltpu.VMEM((stripes * chips, pr, pc), f32)
    part = pltpu.VMEM((stripes * near, pr, pc), f32)
    far = pltpu.VMEM((stripes, pr, pc), f32)
    tile = pltpu.VMEM((8, LANES), f32)
    nsem = stripes * (2 + 2 * (near - 1) + 1 + near // 2 + 1)
    dma = pltpu.SemaphoreType.DMA
    vmem = pl.BlockSpec(memory_space=pltpu.VMEM)
    smem = pl.BlockSpec(memory_space=pltpu.SMEM)
    hbm = pl.BlockSpec(memory_space=pltpu.HBM)
    images, owners, stamps = [pltpu.with_memory_space_constraint(v, pltpu.HBM) for v in (images, owners, stamps)]
    value, coef = pl.pallas_call(
        functools.partial(kernel, count, height, width, stripes),
        out_shape=(
            jax.ShapeDtypeStruct((height, width), f32),
            jax.ShapeDtypeStruct((1, NBASIS + 3), f32),
        ),
        in_specs=[hbm, smem, smem, smem, hbm, hbm],
        out_specs=(vmem,) * 2,
        scratch_shapes=[
            big, big, big, big, part, part, part, part, far, far,
            tile, tile, tile, tile, pltpu.VMEM((near, 8, LANES), f32), tile,
            pltpu.VMEM((width // LANES * height, 3 * LANES), jnp.bfloat16),
            pltpu.VMEM((9, height, width), jnp.bfloat16),
            pltpu.VMEM((NBASIS * height, width), jnp.bfloat16),
            pltpu.VMEM((NBASIS * height, width), f32),
            pltpu.VMEM((width, npix), jnp.bfloat16),
            pltpu.VMEM((LANES, npix), f32),
            pltpu.VMEM((height, width), f32),
            pltpu.VMEM(images.shape, f32),
            pltpu.SMEM(owners.shape, jnp.int32),
            pltpu.VMEM(stamps.shape, jnp.int32), dma((6,)),
            dma((nsem,)), dma((nsem,)), dma((nsem,)), dma((nsem,)), dma((near + 1,)), dma((near + 1,)),
            pltpu.SemaphoreType.REGULAR,
        ],
        compiler_params=pltpu.CompilerParams(
            collective_id=0, has_side_effects=True, vmem_limit_bytes=40 * 1024 * 1024
        ),
    )(images, variance, zero_point, block_mask, owners, stamps)
    return pl.pallas_call(
        finish,
        out_shape=(
            jax.ShapeDtypeStruct((1, height, width), f32),
            jax.ShapeDtypeStruct((1, NBASIS + 3), f32),
        ),
        in_specs=[vmem] * 2,
        out_specs=(hbm,) * 2,
        scratch_shapes=[dma((9,))],
        compiler_params=pltpu.CompilerParams(vmem_limit_bytes=8 * 1024 * 1024),
    )(value, coef)


def solution(mesh):
    in_specs = (
        P(("patch", "epoch"), None, None),
        P(("patch", "epoch")),
        P(("patch", "epoch")),
        P(("patch", "epoch"), None),
        P(("patch", "epoch"), None),
        P("patch"),
    )
    out_specs = (P(("patch", "epoch"), None, None), P(("patch", "epoch"), None))
    return jax.shard_map(shards, mesh=mesh, in_specs=in_specs, out_specs=out_specs, check_vma=False)
```
